768 devices in a mesh: ctx: 96 (over x, z, core), dp: 8 (over y).
Axes of the slice: x: 4, y: 8, z: 12, core: 2. Of those that a mesh axis runs over, the one named last changes fastest.
Arguments:
- queries: bfloat16 [24576, 4096], P('ctx', 'dp'), may hold values from -140 to 140
- keys: bfloat16 [24576, 4096], P('ctx', 'dp'), may hold values from -4.5 to 4.5
- values: bfloat16 [24576, 4096], P('ctx', 'dp'), may hold values from -70 to 70
- doc_ids: int32 [24576], replicated, may hold values from 0 to 7, never falling along the last dimension, each value on 1 to 6144 neighbouring positions
- key_blocks: int32 [192, 6], P('ctx'), may hold values from -1 to 191, as said below
- norm_gain: float32 [4096], P('dp'), may hold values from 0.5 to 1.5
Outputs:
- mixed: bfloat16 [24576, 4096], P('ctx', 'dp')
The draws below stay inside these ranges and needn't reach their ends.
Inputs may be any that keep to these rules, and one draw needn't show every extreme that they name: `key_blocks`: row b lists 6 different blocks, among them b and b - 6, all of them between b - 6 and b; an entry that would lie before block 0 is -1. `doc_ids`: document numbers never fall along the sequence.
All inputs are finite; a program needn't handle non-finite values.
Results may differ from the reference program's by a relative error of at most 0.0048.
Values may be sent and summed in bfloat16 or wider, within the bound.
No kernel may reach another device: no remote copies, remote signals or barrier semaphores. Data moves between devices by JAX's collectives and lax.ppermute only.
A program may use at most 64 MiB of HBM per device.

```python
import math
import jax
import jax.numpy as jnp
import numpy as np
from jax import lax

HEADS = 32
HD = 128
BLK = 128
NB = 6
DOCS = 8
TOKENS = 24576
BPD = 2
NQB = 192
FEAT = 4096


def paired_draw(key):
    base = jax.random.fold_in(key, 11)
    first_key, second_key = jax.random.split(base)
    width = HEADS * HD
    keys_f = jnp.clip(jax.random.normal(first_key, (TOKENS, width), jnp.float32), -4.5, 4.5)
    queries_f = jnp.clip(jax.random.normal(second_key, (TOKENS, width), jnp.float32), -4.5, 4.5)
    return (queries_f, keys_f)


def draw_queries(key, part):
    return paired_draw(key)[0].astype(jnp.bfloat16)


def draw_keys(key, part):
    return paired_draw(key)[1].astype(jnp.bfloat16)


def draw_values(key, part):
    base = jax.random.fold_in(key, 23)
    first_key = jax.random.fold_in(base, 0)
    width = HEADS * HD
    normal_part = jnp.clip(jax.random.normal(first_key, (TOKENS, width), jnp.float32), -4.5, 4.5)
    head_no = (jnp.arange(width) // HD).astype(jnp.float32)
    head_scale = 0.5 * jnp.power(3.0, head_no / max(HEADS - 1, 1))
    drawn = normal_part * head_scale[None, :]
    return drawn.astype(jnp.bfloat16)


def draw_key_blocks(key, part):
    base = jax.random.fold_in(key, 37)
    block_ids = jnp.arange(NQB, dtype=jnp.int32)
    reach = 3 * BPD
    ranks = jax.random.randint(base, (NQB, reach - 1), 0, 1 << 20, dtype=jnp.int32)
    ranks = ranks * reach + jnp.arange(reach - 1, dtype=jnp.int32)[None, :]
    order = jnp.argsort(ranks, axis=1)[:, :NB - 2].astype(jnp.int32) + 1
    offsets = jnp.concatenate([jnp.zeros((NQB, 1), jnp.int32), jnp.full((NQB, 1), reach, jnp.int32), order], axis=1)
    entries = block_ids[:, None] - offsets
    return jnp.where(entries < 0, -1, entries).astype(jnp.int32)


def length_profile(amount, total, most, lean):
    portions = [(1 << 20) // math.isqrt(standing ** lean) + 1 for standing in range(2, amount + 1)]
    rest, counts = total - most - (amount - 1), [1] * (amount - 1)
    while rest > 0:
        free = [i for i in range(amount - 1) if counts[i] < most]
        whole, left = sum([portions[i] for i in free]), rest
        for i in free:
            addition = min(most - counts[i], max(1, left * portions[i] // whole), rest)
            counts[i] = counts[i] + addition
            rest = rest - addition
    return np.array([most] + counts)


def uneven_parts(key, number_of, total, limit, lean):
    if number_of == 2:
        one = jax.random.randint(key, (), max(1, total - limit), min(limit, total - 1) + 1)
        return jnp.stack([one, total - one])
    lengths = jnp.asarray(length_profile(number_of, total, limit, lean), jnp.int32)
    pairs = (number_of - 1) // 2
    source_of, receiver = lengths[1:1 + 2 * pairs:2], lengths[2:2 + 2 * pairs:2]
    room = jnp.minimum(source_of - 1, limit - receiver)
    moved = jax.random.randint(jax.random.fold_in(key, 1), (pairs,), 0, 1 << 20) % (room + 1)
    lengths = lengths.at[1:1 + 2 * pairs:2].set(source_of - moved).at[2:2 + 2 * pairs:2].set(receiver + moved)
    return lengths[jax.random.permutation(jax.random.fold_in(key, 2), number_of)]


def setup_inputs(seed: int = 0) -> dict:
    streams_of = jax.random.split(jax.random.key(seed), 7)
    return {
        "queries": draw_queries(jax.random.fold_in(streams_of[6], 71), 0),
        "keys": draw_keys(jax.random.fold_in(streams_of[6], 71), 0),
        "values": draw_values(jax.random.fold_in(streams_of[6], 71), 0),
        "doc_ids": jnp.searchsorted(jnp.cumsum(uneven_parts(streams_of[3], DOCS, TOKENS, TOKENS // 4, 0)), jnp.arange(TOKENS), side="right").astype(jnp.int32),
        "key_blocks": draw_key_blocks(jax.random.fold_in(streams_of[6], 71), 0),
        "norm_gain": jnp.clip(1.0 + 0.1 * jax.random.normal(streams_of[5], (FEAT,), jnp.float32), 0.5, 1.5),
    }


def linear_part(q_all, k_all, v_all, d_all):

    def advance(carry, pieces):
        carry_doc, carried = carry
        q_block, k_block, v_block, d_block = pieces
        q_float = q_block.astype(jnp.float32)
        k_float = k_block.astype(jnp.float32)
        v_float = v_block.astype(jnp.float32)
        block_last = d_block[-1]
        rounded = lax.optimization_barrier(carried.astype(jnp.bfloat16)).astype(jnp.float32)
        inner = jnp.einsum('thd,hde->the', q_float, rounded) * (d_block == carry_doc).astype(jnp.float32)[:, None, None]
        places = jnp.arange(d_block.shape[0])
        allowed = (places[:, None] >= places[None, :]) & (d_block[:, None] == d_block[None, :])
        local_scores = jnp.einsum('thd,shd->hts', q_float, k_float)
        local_scores = jnp.where(allowed[None], local_scores, 0.0)
        local_scores = lax.optimization_barrier(local_scores.astype(jnp.bfloat16)).astype(jnp.float32)
        intra = jnp.einsum('hts,she->the', local_scores, v_float)
        keep_rows = (d_block == block_last).astype(jnp.float32)
        update = jnp.einsum('thd,the->hde', k_float, v_float * keep_rows[:, None, None])
        carried = jnp.where(carry_doc == block_last, carried, 0.0) + update
        return ((block_last, carried), inner + intra)
    start = (jnp.int32(-1), jnp.zeros((HEADS, HD, HD), jnp.float32))
    _, outputs = lax.scan(advance, start, (q_all, k_all, v_all, d_all))
    return outputs

def reference(queries, keys, values, doc_ids, key_blocks, norm_gain):
    q_all = queries.reshape(NQB, BLK, HEADS, HD)
    k_all = keys.reshape(NQB, BLK, HEADS, HD)
    v_all = values.reshape(NQB, BLK, HEADS, HD)
    d_all = doc_ids.reshape(NQB, BLK)
    linear_all = linear_part(q_all, k_all, v_all, d_all)
    scale = 1.0 / math.sqrt(HD)

    def finish(pieces):
        q_block, listed, block_index, lin_block = pieces
        present = listed >= 0
        chosen = jnp.where(present, listed, 0).astype(jnp.int32)
        key_sel = k_all[chosen].reshape(NB * BLK, HEADS, HD).astype(jnp.float32)
        value_sel = v_all[chosen].reshape(NB * BLK, HEADS, HD).astype(jnp.float32)
        key_pos = (chosen[:, None] * BLK + jnp.arange(BLK, dtype=jnp.int32)[None, :]).reshape(-1)
        key_doc = doc_ids[key_pos]
        key_live = jnp.repeat(present, BLK)
        query_pos = block_index * BLK + jnp.arange(BLK, dtype=jnp.int32)
        query_doc = doc_ids[query_pos]
        allowed = key_live[None, :] & (key_doc[None, :] == query_doc[:, None]) & (key_pos[None, :] <= query_pos[:, None])
        scores = jnp.einsum('thd,shd->hts', q_block.astype(jnp.float32), key_sel) * scale
        scores = jnp.where(allowed[None], scores, -jnp.inf)
        top = lax.optimization_barrier(jnp.max(scores, axis=-1, keepdims=True))
        expo = jnp.exp(scores - top)
        weights = expo / lax.optimization_barrier(jnp.sum(expo, axis=-1, keepdims=True))
        weights = lax.optimization_barrier(weights.astype(jnp.bfloat16)).astype(jnp.float32)
        soft = jnp.einsum('hts,she->the', weights, value_sel)
        squares = lax.optimization_barrier(jnp.sum(lin_block * lin_block, axis=(1, 2)))
        inverse = lax.rsqrt(squares / (HEADS * HD) + 1e-06)
        normed = (lin_block * inverse[:, None, None]).reshape(BLK, HEADS * HD) * norm_gain
        return (normed + soft.reshape(BLK, HEADS * HD)).astype(jnp.bfloat16)
    block_ids = jnp.arange(NQB, dtype=jnp.int32)
    result = lax.map(finish, (q_all, key_blocks, block_ids, linear_all))
    return result.reshape(TOKENS, HEADS * HD)
```

```python
import functools
import math

import jax
import jax.numpy as jnp
from jax import lax
from jax.experimental import pallas as pl
from jax.experimental.pallas import tpu as pltpu
from jax.sharding import PartitionSpec as P

HEADS = 32
HD = 128
BLK = 128
NB = 6
ROW = 24
PIECE = 24
NEG = -1e30
F32 = jnp.float32
BF16 = jnp.bfloat16
VM = pl.BlockSpec(memory_space=pltpu.VMEM)
SM = pl.BlockSpec(memory_space=pltpu.SMEM)


def call(body, outs, ins, name):
    return pl.pallas_call(
        body,
        out_shape=outs,
        in_specs=ins,
        out_specs=jax.tree.map(lambda _: VM, outs),
        name=name,
    )


def dot_nn(a, b):
    return lax.dot_general(a, b, (((1,), (0,)), ((), ())), preferred_element_type=F32)


def dot_nt(a, b):
    return lax.dot_general(a, b, (((1,), (1,)), ((), ())), preferred_element_type=F32)


def dot_tn(a, b):
    return lax.dot_general(a, b, (((0,), (0,)), ((), ())), preferred_element_type=F32)


def doc_row(doc_ref, row):
    return doc_ref[pl.ds(row, 1), :].astype(F32)


def down(row):
    return jnp.broadcast_to(row, (BLK, BLK)).T


def count_below(row, value):
    return jnp.sum(jnp.where(row < value, 1.0, 0.0), axis=1, keepdims=True)


def head(h):
    return slice(h * HD, (h + 1) * HD)


def summary_kernel(doc_ref, k_ref, v_ref, state_ref, kv_ref):
    me = lax.axis_index("ctx")
    d0, d1 = doc_row(doc_ref, 2 * me), doc_row(doc_ref, 2 * me + 1)
    last = d1[:, BLK - 1 :]
    first = count_below(d0, last) + count_below(d1, last)
    rows = lax.broadcasted_iota(jnp.int32, (2 * BLK, HD), 0).astype(F32)
    keep = rows >= first
    for h in range(4):
        vm = jnp.where(keep, v_ref[:, head(h)].astype(F32), 0.0).astype(BF16)
        state_ref[head(h), :] = dot_tn(k_ref[:, head(h)], vm).astype(BF16)
    state_ref[4 * HD :, :] = jnp.zeros((ROW * PIECE - 4 * HD, HD), BF16)
    kv_ref[: 2 * BLK, :] = k_ref[...]
    kv_ref[2 * BLK :, :] = v_ref[...]


def row_docs(doc_ref):
    row = lax.axis_index("ctx") // ROW
    docs = doc_ref[pl.ds(pl.multiple_of(row * 2 * ROW, 8), 2 * ROW), :].astype(F32)
    return row, jnp.broadcast_to(docs[:, BLK - 1 :], (2 * ROW, HD))


def total_kernel(doc_ref, piece_ref, total_ref):
    _, docs = row_docs(doc_ref)
    last = docs[2 * ROW - 1 :, :]
    total = jnp.zeros((PIECE, HD), F32)
    for j in range(ROW):
        same = docs[2 * j + 1 : 2 * j + 2, :] == last
        total += jnp.where(same, piece_ref[j].astype(F32), 0.0)
    total_ref[...] = total


def prefix_kernel(doc_ref, piece_ref, carry_ref, before_ref):
    row, docs = row_docs(doc_ref)
    past = doc_row(doc_ref, jnp.maximum(2 * ROW * row - 1, 0))
    before = jnp.broadcast_to(past[:, BLK - 1 :], (1, HD))
    running = carry_ref[...]
    for j in range(ROW):
        before_ref[j] = running.astype(BF16)
        now = docs[2 * j + 1 : 2 * j + 2, :]
        running = jnp.where(now == before, running, 0.0) + piece_ref[j].astype(F32)
        before = now


def linear_kernel(doc_ref, q_ref, k_ref, v_ref, state_ref, lin_ref, sq_ref):
    me = lax.axis_index("ctx")
    past = doc_row(doc_ref, jnp.maximum(2 * me - 1, 0))[:, BLK - 1 :]
    lane = lax.broadcasted_iota(jnp.int32, (BLK, BLK), 1)
    line = lax.broadcasted_iota(jnp.int32, (BLK, BLK), 0)
    causal = lane <= line
    docs = [doc_row(doc_ref, 2 * me), doc_row(doc_ref, 2 * me + 1)]
    lasts = [docs[0][:, BLK - 1 :], docs[1][:, BLK - 1 :]]
    cols = [down(docs[0]), down(docs[1])]
    keep = cols[0] == lasts[0]
    squares = [jnp.zeros((BLK, HD), F32), jnp.zeros((BLK, HD), F32)]
    for h in range(4):
        state = state_ref[head(h), :]
        for t in range(2):
            rows = slice(t * BLK, (t + 1) * BLK)
            q, k, v = q_ref[rows, head(h)], k_ref[rows, head(h)], v_ref[rows, head(h)]
            inner = jnp.where(cols[t] == past if t == 0 else cols[t] == lasts[0], dot_nn(q, state), 0.0)
            scores = jnp.where(causal & (cols[t] == docs[t]), dot_nt(q, k), 0.0).astype(BF16)
            lin = inner + dot_nn(scores, v)
            lin_ref[rows, head(h)] = lin
            squares[t] += lin * lin
            if t == 0:
                update = dot_tn(k, jnp.where(keep, v.astype(F32), 0.0).astype(BF16))
                state = (jnp.where(past == lasts[0], state.astype(F32), 0.0) + update).astype(BF16)
    sums = [jnp.sum(square.T, axis=0, keepdims=True) for square in squares]
    row = lax.broadcasted_iota(jnp.int32, (8, BLK), 0)
    tile = jnp.where(row == 0, sums[0], jnp.where(row == 1, sums[1], 0.0))
    for place in range(sq_ref.shape[0]):
        sq_ref[place] = tile


def soft_kernel(list_ref, doc_ref, q_ref, kv0_ref, kv1_ref, kv2_ref, kv3_ref, soft_ref):
    me = lax.axis_index("ctx")
    base = 2 * me - NB
    lane = lax.broadcasted_iota(jnp.int32, (BLK, BLK), 1)
    line = lax.broadcasted_iota(jnp.int32, (BLK, BLK), 0)
    causal = lane <= line
    docs = [doc_row(doc_ref, jnp.maximum(base + w, 0)) for w in range(8)]
    scale = 1.0 / math.sqrt(HD)
    allowed = []
    for t in range(2):
        col = down(docs[NB + t])
        for w in range(8):
            if w < t or w > NB + t:
                allowed.append(None)
                continue
            block = base + w
            listed = list_ref[t, 0] == block
            for n in range(1, NB):
                listed = listed | (list_ref[t, n] == block)
            listed = listed & (block >= 0)
            match = col == jnp.where(listed, docs[w], -1.0)
            allowed.append(match & causal if w == NB + t else match)
    kvs = [kv3_ref, kv2_ref, kv1_ref, kv0_ref]
    for h in range(4):
        q = q_ref[:, head(h)]
        raw = [dot_nt(q, kv[: 2 * BLK, head(h)]) for kv in kvs]
        weights = [[], []]
        for t in range(2):
            rows = slice(t * BLK, (t + 1) * BLK)
            pieces = []
            for w in range(8):
                mask = allowed[8 * t + w]
                if mask is None:
                    pieces.append(None)
                    continue
                piece = raw[w // 2][rows, (w % 2) * BLK : (w % 2 + 1) * BLK]
                pieces.append(jnp.where(mask, piece, NEG))
            live = [piece for piece in pieces if piece is not None]
            top = jnp.max(functools.reduce(jnp.maximum, live), axis=1, keepdims=True)
            expos = [None if piece is None else jnp.exp((piece - top) * scale) for piece in pieces]
            total = jnp.sum(sum(e for e in expos if e is not None), axis=1, keepdims=True)
            share = 1.0 / total
            weights[t] = [
                jnp.zeros((BLK, BLK), BF16) if e is None else (e * share).astype(BF16) for e in expos
            ]
        out = jnp.zeros((2 * BLK, HD), F32)
        for d in range(4):
            both = jnp.concatenate(
                [jnp.concatenate([weights[t][2 * d], weights[t][2 * d + 1]], axis=1) for t in range(2)],
                axis=0,
            )
            out += dot_nn(both, kvs[d][2 * BLK :, head(h)])
        soft_ref[:, head(h)] = out


def mix_kernel(lin_ref, soft_ref, sq_ref, gain_ref, out_ref):
    total = jnp.sum(sq_ref[...], axis=0)
    inverse = lax.rsqrt(total / (HEADS * HD) + 1e-06)
    for t in range(2):
        rows = slice(t * BLK, (t + 1) * BLK)
        col = down(inverse[t : t + 1, :])
        for h in range(4):
            normed = lin_ref[rows, head(h)] * col * gain_ref[:, head(h)]
            out_ref[rows, head(h)] = (normed + soft_ref[rows, head(h)]).astype(BF16)


def local(queries, keys, values, doc_ids, key_blocks, norm_gain):
    tok_rows, feat_width = queries.shape
    devices = lax.axis_size("ctx")
    parts = lax.axis_size("dp")
    docs = doc_ids.reshape(-1, BLK)
    gain = norm_gain.reshape(1, feat_width)
    shape = jax.ShapeDtypeStruct
    groups = [list(range(first, first + ROW)) for first in range(0, devices, ROW)]

    def shifted(x, by):
        return lax.ppermute(x, "ctx", [(i, i + by) for i in range(devices - by)])

    def exchange(x):
        return lax.all_to_all(x, "ctx", 0, 0, axis_index_groups=groups)

    summary, kv = call(
        summary_kernel,
        (shape((ROW * PIECE, HD), BF16), shape((2 * tok_rows, feat_width), BF16)),
        [VM, VM, VM],
        "summary",
    )(docs, keys, values)
    kv1 = shifted(kv, 1)
    pieces = exchange(summary.reshape(ROW, PIECE, HD))
    kv2 = shifted(kv1, 1)
    total = call(total_kernel, shape((PIECE, HD), F32), [VM, VM], "total")(docs, pieces)
    carry = shifted(total, ROW)
    before = call(prefix_kernel, shape((ROW, PIECE, HD), BF16), [VM, VM, VM], "prefix")(
        docs, pieces, carry
    )
    kv3 = shifted(kv2, 1)
    state = exchange(before).reshape(ROW * PIECE, HD)
    lin, squares = call(
        linear_kernel,
        (shape((tok_rows, feat_width), F32), shape((parts, 8, BLK), F32)),
        [VM] * 5,
        "linear",
    )(docs, queries, keys, values, state)
    squares = lax.all_to_all(squares, "dp", 0, 0)
    soft = call(soft_kernel, shape((tok_rows, feat_width), F32), [SM] + [VM] * 6, "soft")(
        key_blocks, docs, queries, kv, kv1, kv2, kv3
    )
    return call(mix_kernel, shape((tok_rows, feat_width), BF16), [VM] * 4, "mix")(
        lin, soft, squares, gain
    )


def solution(mesh):
    return jax.shard_map(
        local,
        mesh=mesh,
        in_specs=(P("ctx", "dp"), P("ctx", "dp"), P("ctx", "dp"), P(), P("ctx", None), P("dp")),
        out_specs=P("ctx", "dp"),
        check_vma=False,
    )
```

```python
import functools
import math

import jax
import jax.numpy as jnp
from jax import lax
from jax.experimental import pallas as pl
from jax.experimental.pallas import tpu as pltpu
from jax.sharding import PartitionSpec as P


HEADS = 32
HD = 128
BLK = 128
NB = 6
ROW = 24
PIECE = 24
NEG = -1e30
F32 = jnp.float32
BF16 = jnp.bfloat16
VM = pl.BlockSpec(memory_space=pltpu.VMEM)
SM = pl.BlockSpec(memory_space=pltpu.SMEM)


def call(body, outs, *operands):
    smem = [x.shape == (2, NB) for x in operands]
    operands = [
        x if small else pltpu.with_memory_space_constraint(x, pltpu.VMEM)
        for x, small in zip(operands, smem)
    ]
    return pl.pallas_call(
        body,
        out_shape=outs,
        in_specs=[SM if small else VM for small in smem],
        out_specs=jax.tree.map(lambda _: VM, outs),
        compiler_params=pltpu.CompilerParams(vmem_limit_bytes=12 << 20),
    )(*operands)


def dot_nn(a, b):
    return lax.dot_general(a, b, (((1,), (0,)), ((), ())), preferred_element_type=F32)


def dot_nt(a, b):
    return lax.dot_general(a, b, (((1,), (1,)), ((), ())), preferred_element_type=F32)


def dot_tn(a, b):
    return lax.dot_general(a, b, (((0,), (0,)), ((), ())), preferred_element_type=F32)


def doc_row(doc_ref, row):
    return doc_ref[pl.ds(row, 1), :].astype(F32)


def down(row):
    return jnp.broadcast_to(row, (BLK, BLK)).T


def count_below(row, value):
    return jnp.sum(jnp.where(row < value, 1.0, 0.0), axis=1, keepdims=True)


def head(h):
    return slice(h * HD, (h + 1) * HD)


def summary_kernel(doc_ref, k_ref, v_ref, state_ref, kv_ref):
    me = lax.axis_index("ctx")
    d0, d1 = doc_row(doc_ref, 2 * me), doc_row(doc_ref, 2 * me + 1)
    last = d1[:, BLK - 1 :]
    first = count_below(d0, last) + count_below(d1, last)
    rows = lax.broadcasted_iota(jnp.int32, (2 * BLK, HD), 0).astype(F32)
    keep = rows >= first
    for h in range(4):
        vm = jnp.where(keep, v_ref[:, head(h)].astype(F32), 0.0).astype(BF16)
        state_ref[head(h), :] = dot_tn(k_ref[:, head(h)], vm).astype(BF16)
    state_ref[4 * HD :, :] = jnp.zeros((ROW * PIECE - 4 * HD, HD), BF16)
    kv_ref[: 2 * BLK, :] = k_ref[...]
    kv_ref[2 * BLK :, :] = v_ref[...]


def row_docs(doc_ref):
    row = lax.axis_index("ctx") // ROW
    docs = doc_ref[pl.ds(pl.multiple_of(row * 2 * ROW, 8), 2 * ROW), :].astype(F32)
    return row, jnp.broadcast_to(docs[:, BLK - 1 :], (2 * ROW, HD))


def total_kernel(doc_ref, piece_ref, total_ref):
    _, docs = row_docs(doc_ref)
    last = docs[2 * ROW - 1 :, :]
    total = jnp.zeros((PIECE, HD), F32)
    for j in range(ROW):
        same = docs[2 * j + 1 : 2 * j + 2, :] == last
        total += jnp.where(same, piece_ref[j].astype(F32), 0.0)
    total_ref[...] = total


def prefix_kernel(doc_ref, piece_ref, carry_ref, before_ref):
    row, docs = row_docs(doc_ref)
    past = doc_row(doc_ref, jnp.maximum(2 * ROW * row - 1, 0))
    before = jnp.broadcast_to(past[:, BLK - 1 :], (1, HD))
    running = carry_ref[...]
    for j in range(ROW):
        before_ref[j] = running.astype(BF16)
        now = docs[2 * j + 1 : 2 * j + 2, :]
        running = jnp.where(now == before, running, 0.0) + piece_ref[j].astype(F32)
        before = now


def inside_kernel(doc_ref, q_ref, k_ref, v_ref, intra_ref, update_ref):
    me = lax.axis_index("ctx")
    lane = lax.broadcasted_iota(jnp.int32, (BLK, BLK), 1)
    line = lax.broadcasted_iota(jnp.int32, (BLK, BLK), 0)
    causal = lane <= line
    docs = [doc_row(doc_ref, 2 * me), doc_row(doc_ref, 2 * me + 1)]
    cols = [down(docs[0]), down(docs[1])]
    keep = cols[0] == docs[0][:, BLK - 1 :]
    for h in range(4):
        for t in range(2):
            rows = slice(t * BLK, (t + 1) * BLK)
            q, k, v = q_ref[rows, head(h)], k_ref[rows, head(h)], v_ref[rows, head(h)]
            scores = jnp.where(causal & (cols[t] == docs[t]), dot_nt(q, k), 0.0).astype(BF16)
            intra_ref[rows, head(h)] = dot_nn(scores, v)
            if t == 0:
                kept = jnp.where(keep, v.astype(F32), 0.0).astype(BF16)
                update_ref[head(h), :] = dot_tn(k, kept)


def linear_kernel(doc_ref, q_ref, intra_ref, update_ref, state_ref, lin_ref, sq_ref):
    me = lax.axis_index("ctx")
    past = doc_row(doc_ref, jnp.maximum(2 * me - 1, 0))[:, BLK - 1 :]
    docs = [doc_row(doc_ref, 2 * me), doc_row(doc_ref, 2 * me + 1)]
    mid = docs[0][:, BLK - 1 :]
    live = [down(docs[0]) == past, down(docs[1]) == mid]
    squares = [jnp.zeros((BLK, HD), F32), jnp.zeros((BLK, HD), F32)]
    for h in range(4):
        first = state_ref[head(h), :]
        second = (jnp.where(past == mid, first.astype(F32), 0.0) + update_ref[head(h), :]).astype(BF16)
        for t, state in enumerate((first, second)):
            rows = slice(t * BLK, (t + 1) * BLK)
            inner = jnp.where(live[t], dot_nn(q_ref[rows, head(h)], state), 0.0)
            lin = inner + intra_ref[rows, head(h)]
            lin_ref[rows, head(h)] = lin
            squares[t] += lin * lin
    sums = [jnp.sum(square.T, axis=0, keepdims=True) for square in squares]
    row = lax.broadcasted_iota(jnp.int32, (8, BLK), 0)
    tile = jnp.where(row == 0, sums[0], jnp.where(row == 1, sums[1], 0.0))
    for place in range(sq_ref.shape[0]):
        sq_ref[place] = tile


def soft_parts(list_ref, doc_ref, q_ref, kvs, windows, merge):
    me = lax.axis_index("ctx")
    base = 2 * me - NB
    lane = lax.broadcasted_iota(jnp.int32, (BLK, BLK), 1)
    line = lax.broadcasted_iota(jnp.int32, (BLK, BLK), 0)
    causal = lane <= line
    scale = 1.0 / math.sqrt(HD)
    masks = []
    for t in range(2):
        col = down(doc_row(doc_ref, base + NB + t))
        mine = []
        for w in windows:
            if w < t or w > NB + t:
                mine.append(None)
                continue
            block = base + w
            listed = list_ref[t, 0] == block
            for n in range(1, NB):
                listed = listed | (list_ref[t, n] == block)
            listed = listed & (block >= 0)
            row = doc_row(doc_ref, jnp.maximum(block, 0))
            match = col == jnp.where(listed, row, -1.0)
            mine.append(match & causal if w == NB + t else match)
        masks.append(mine)
    for h in range(4):
        q = q_ref[:, head(h)]
        raw = [dot_nt(q, kv[: 2 * BLK, head(h)]) for kv in kvs]
        tops, sums, parts = [], [], []
        for t in range(2):
            rows = slice(t * BLK, (t + 1) * BLK)
            pieces = []
            for n, mask in enumerate(masks[t]):
                if mask is None:
                    pieces.append(None)
                else:
                    piece = raw[n // 2][rows, (n % 2) * BLK : (n % 2 + 1) * BLK]
                    pieces.append(jnp.where(mask, piece, NEG))
            live = [piece for piece in pieces if piece is not None]
            top = jnp.max(functools.reduce(jnp.maximum, live), axis=1, keepdims=True)
            top = jnp.maximum(top, merge.top(h, t))
            expos = [None if piece is None else jnp.exp((piece - top) * scale) for piece in pieces]
            total = jnp.sum(sum(e for e in expos if e is not None), axis=1, keepdims=True)
            zero = jnp.zeros((BLK, BLK), BF16)
            parts.append([zero if e is None else e.astype(BF16) for e in expos])
            tops.append(top)
            sums.append(total)
        out = jnp.zeros((2 * BLK, HD), F32)
        for d, kv in enumerate(kvs):
            both = jnp.concatenate(
                [jnp.concatenate(parts[t][2 * d : 2 * d + 2], axis=1) for t in range(2)], axis=0
            )
            out += dot_nn(both, kv[2 * BLK :, head(h)])
        for t in range(2):
            merge.store(h, t, tops[t], sums[t], out[t * BLK : (t + 1) * BLK], scale)


class Near:
    def __init__(self, acc_ref, stat_ref):
        self.acc, self.stat = acc_ref, stat_ref

    def top(self, h, t):
        return NEG

    def store(self, h, t, top, total, out, scale):
        rows = slice(t * BLK, (t + 1) * BLK)
        self.acc[rows, head(h)] = out
        self.stat[rows, h : h + 1] = top
        self.stat[rows, 4 + h : 5 + h] = total


class Far(Near):
    def __init__(self, acc_ref, stat_ref, soft_ref):
        self.acc, self.stat, self.soft = acc_ref, stat_ref, soft_ref

    def top(self, h, t):
        return self.stat[t * BLK : (t + 1) * BLK, h : h + 1]

    def store(self, h, t, top, total, out, scale):
        rows = slice(t * BLK, (t + 1) * BLK)
        fade = jnp.exp((self.top(h, t) - top) * scale)
        share = 1.0 / (self.stat[rows, 4 + h : 5 + h] * fade + total)
        self.soft[rows, head(h)] = (self.acc[rows, head(h)] * fade + out) * share


def near_kernel(list_ref, doc_ref, q_ref, kv0_ref, kv1_ref, acc_ref, stat_ref):
    soft_parts(list_ref, doc_ref, q_ref, [kv1_ref, kv0_ref], (4, 5, 6, 7), Near(acc_ref, stat_ref))


def far_kernel(list_ref, doc_ref, q_ref, kv2_ref, kv3_ref, acc_ref, stat_ref, soft_ref):
    far = Far(acc_ref, stat_ref, soft_ref)
    soft_parts(list_ref, doc_ref, q_ref, [kv3_ref, kv2_ref], (0, 1, 2, 3), far)


def mix_kernel(lin_ref, soft_ref, sq_ref, gain_ref, out_ref):
    total = jnp.sum(sq_ref[...], axis=0)
    inverse = lax.rsqrt(total / (HEADS * HD) + 1e-06)
    for t in range(2):
        rows = slice(t * BLK, (t + 1) * BLK)
        col = down(inverse[t : t + 1, :])
        for h in range(4):
            normed = lin_ref[rows, head(h)] * col * gain_ref[:, head(h)]
            out_ref[rows, head(h)] = (normed + soft_ref[rows, head(h)]).astype(BF16)


def local(queries, keys, values, doc_ids, key_blocks, norm_gain):
    tok_rows, feat_width = queries.shape
    devices = lax.axis_size("ctx")
    parts = lax.axis_size("dp")
    docs = doc_ids.reshape(-1, BLK)
    gain = norm_gain.reshape(1, feat_width)
    groups = [list(range(first, first + ROW)) for first in range(0, devices, ROW)]
    wide = pltpu.VMEM((tok_rows, feat_width), F32)

    def shifted(x, by):
        return lax.ppermute(x, "ctx", [(i, i + by) for i in range(devices - by)])

    def exchange(x):
        return lax.all_to_all(x, "ctx", 0, 0, axis_index_groups=groups)

    pieces_shape = pltpu.VMEM((ROW, PIECE, HD), BF16)
    summary, kv = call(
        summary_kernel,
        (pltpu.VMEM((ROW * PIECE, HD), BF16), pltpu.VMEM((2 * tok_rows, feat_width), BF16)),
        docs,
        keys,
        values,
    )
    pieces = exchange(summary.reshape(ROW, PIECE, HD))
    kv1 = shifted(kv, 1)
    intra, update = call(
        inside_kernel, (wide, pltpu.VMEM((feat_width, HD), F32)), docs, queries, keys, values
    )
    total = call(total_kernel, pltpu.VMEM((PIECE, HD), F32), docs, pieces)
    carry = shifted(total, ROW)
    kv2 = shifted(kv1, 1)
    before = call(prefix_kernel, pieces_shape, docs, pieces, carry)
    state = exchange(before).reshape(ROW * PIECE, HD)
    kv3 = shifted(kv2, 1)
    near = call(near_kernel, (wide, pltpu.VMEM((tok_rows, HD), F32)), key_blocks, docs, queries, kv, kv1)
    lin, squares = call(
        linear_kernel, (wide, pltpu.VMEM((parts, 8, BLK), F32)), docs, queries, intra, update, state
    )
    squares = lax.all_to_all(squares, "dp", 0, 0)
    soft = call(far_kernel, wide, key_blocks, docs, queries, kv2, kv3, *near)
    return call(
        mix_kernel, jax.ShapeDtypeStruct((tok_rows, feat_width), BF16), lin, soft, squares, gain
    )


def solution(mesh):
    return jax.shard_map(
        local,
        mesh=mesh,
        in_specs=(P("ctx", "dp"), P("ctx", "dp"), P("ctx", "dp"), P(), P("ctx", None), P("dp")),
        out_specs=P("ctx", "dp"),
        check_vma=False,
    )
```

```python
import functools
import math

import jax
import jax.numpy as jnp
from jax import lax
from jax.experimental import pallas as pl
from jax.experimental.pallas import tpu as pltpu
from jax.sharding import PartitionSpec as P


HEADS = 32
HD = 128
BLK = 128
NB = 6
ROW = 24
PIECE = 24
NEG = -1e30
F32 = jnp.float32
BF16 = jnp.bfloat16
VM = pl.BlockSpec(memory_space=pltpu.VMEM)
SM = pl.BlockSpec(memory_space=pltpu.SMEM)


def call(body, outs, *operands, scratch=None, aliases=None):
    small = [x.shape == (2, NB) for x in operands]
    if scratch is not None:
        specs = [pl.BlockSpec(memory_space=pltpu.HBM)] * len(operands)
        operands = [pltpu.with_memory_space_constraint(x, pltpu.HBM) for x in operands]
    else:
        specs = [SM if flag else VM for flag in small]
        operands = [
            x if flag else pltpu.with_memory_space_constraint(x, pltpu.VMEM)
            for x, flag in zip(operands, small)
        ]
    return pl.pallas_call(
        body,
        out_shape=outs,
        in_specs=specs,
        out_specs=jax.tree.map(lambda _: VM, outs),
        scratch_shapes=scratch or (),
        input_output_aliases=aliases or {},
        compiler_params=pltpu.CompilerParams(vmem_limit_bytes=12 << 20),
    )(*operands)


def dot_nn(a, b):
    return lax.dot_general(a, b, (((1,), (0,)), ((), ())), preferred_element_type=F32)


def dot_nt(a, b):
    return lax.dot_general(a, b, (((1,), (1,)), ((), ())), preferred_element_type=F32)


def dot_tn(a, b):
    return lax.dot_general(a, b, (((0,), (0,)), ((), ())), preferred_element_type=F32)


def doc_row(doc_ref, row):
    return doc_ref[pl.ds(row, 1), :].astype(F32)


def down(row):
    return jnp.broadcast_to(row, (BLK, BLK)).T


def count_below(row, value):
    return jnp.sum(jnp.where(row < value, 1.0, 0.0), axis=1, keepdims=True)


def head(h):
    return slice(h * HD, (h + 1) * HD)


def summary_kernel(doc_hbm, k_hbm, v_hbm, state_ref, kv_ref, doc_ref, sems):
    me = lax.axis_index("ctx")
    tok = k_hbm.shape[0]
    group = pl.multiple_of((2 * me // 8) * 8, 8)
    copies = [
        pltpu.make_async_copy(doc_hbm.at[pl.ds(group, 8), :], doc_ref, sems.at[0]),
        pltpu.make_async_copy(k_hbm, kv_ref.at[:tok], sems.at[1]),
        pltpu.make_async_copy(v_hbm, kv_ref.at[tok:], sems.at[2]),
    ]
    for copy in copies:
        copy.start()
    state_ref[4 * HD :, :] = jnp.zeros((ROW * PIECE - 4 * HD, HD), BF16)
    copies[0].wait()
    d0, d1 = doc_row(doc_ref, 2 * me - group), doc_row(doc_ref, 2 * me - group + 1)
    last = d1[:, BLK - 1 :]
    first = count_below(d0, last) + count_below(d1, last)
    rows = lax.broadcasted_iota(jnp.int32, (tok, HD), 0).astype(F32)
    keep = rows >= first
    copies[1].wait()
    copies[2].wait()
    for h in range(4):
        vm = jnp.where(keep, kv_ref[tok:, head(h)].astype(F32), 0.0).astype(BF16)
        state_ref[head(h), :] = dot_tn(kv_ref[:tok, head(h)], vm).astype(BF16)


def row_docs(doc_ref):
    row = lax.axis_index("ctx") // ROW
    docs = doc_ref[pl.ds(pl.multiple_of(row * 2 * ROW, 8), 2 * ROW), :].astype(F32)
    return row, jnp.broadcast_to(docs[:, BLK - 1 :], (2 * ROW, HD))


def total_kernel(doc_ref, piece_ref, total_ref):
    _, docs = row_docs(doc_ref)
    last = docs[2 * ROW - 1 :, :]
    total = jnp.zeros((PIECE, HD), F32)
    for j in range(ROW):
        same = docs[2 * j + 1 : 2 * j + 2, :] == last
        total += jnp.where(same, piece_ref[j].astype(F32), 0.0)
    total_ref[...] = total


def prefix_kernel(doc_ref, piece_ref, carry_ref, before_ref):
    row, docs = row_docs(doc_ref)
    past = doc_row(doc_ref, jnp.maximum(2 * ROW * row - 1, 0))
    before = jnp.broadcast_to(past[:, BLK - 1 :], (1, HD))
    running = carry_ref[...]
    for j in range(ROW):
        before_ref[j] = running.astype(BF16)
        now = docs[2 * j + 1 : 2 * j + 2, :]
        running = jnp.where(now == before, running, 0.0) + piece_ref[j].astype(F32)
        before = now


def linear_kernel(doc_ref, q_ref, intra_ref, update_ref, state_ref, lin_ref, sq_ref):
    me = lax.axis_index("ctx")
    past = doc_row(doc_ref, jnp.maximum(2 * me - 1, 0))[:, BLK - 1 :]
    docs = [doc_row(doc_ref, 2 * me), doc_row(doc_ref, 2 * me + 1)]
    mid = docs[0][:, BLK - 1 :]
    live = [down(docs[0]) == past, down(docs[1]) == mid]
    squares = [jnp.zeros((BLK, HD), F32), jnp.zeros((BLK, HD), F32)]
    for h in range(4):
        first = state_ref[head(h), :]
        second = (jnp.where(past == mid, first.astype(F32), 0.0) + update_ref[head(h), :]).astype(BF16)
        for t, state in enumerate((first, second)):
            rows = slice(t * BLK, (t + 1) * BLK)
            inner = jnp.where(live[t], dot_nn(q_ref[rows, head(h)], state), 0.0)
            lin = inner + intra_ref[rows, head(h)]
            lin_ref[rows, head(h)] = lin
            squares[t] += lin * lin
    sums = [jnp.sum(square.T, axis=0, keepdims=True) for square in squares]
    row = lax.broadcasted_iota(jnp.int32, (8, BLK), 0)
    tile = jnp.where(row == 0, sums[0], jnp.where(row == 1, sums[1], 0.0))
    for place in range(sq_ref.shape[0]):
        sq_ref[place] = tile


def soft_parts(list_ref, doc_ref, q_ref, kvs, windows, merge, own=None):
    me = lax.axis_index("ctx")
    base = 2 * me - NB
    lane = lax.broadcasted_iota(jnp.int32, (BLK, BLK), 1)
    line = lax.broadcasted_iota(jnp.int32, (BLK, BLK), 0)
    causal = lane <= line
    scale = 1.0 / math.sqrt(HD)
    masks = []
    for t in range(2):
        col = down(doc_row(doc_ref, base + NB + t))
        mine = []
        for w in windows:
            if w < t or w > NB + t:
                mine.append(None)
                continue
            block = base + w
            listed = list_ref[t, 0] == block
            for n in range(1, NB):
                listed = listed | (list_ref[t, n] == block)
            listed = listed & (block >= 0)
            row = doc_row(doc_ref, jnp.maximum(block, 0))
            match = col == jnp.where(listed, row, -1.0)
            mine.append(match & causal if w == NB + t else match)
        masks.append(mine)
    for h in range(4):
        q = q_ref[:, head(h)]
        raw = [dot_nt(q, k_ref[:, head(h)]) for k_ref, _ in kvs]
        if own is not None:
            own(h, raw[0])
        tops, sums, parts = [], [], []
        for t in range(2):
            rows = slice(t * BLK, (t + 1) * BLK)
            pieces = []
            for n, mask in enumerate(masks[t]):
                if mask is None:
                    pieces.append(None)
                else:
                    piece = raw[n // 2][rows, (n % 2) * BLK : (n % 2 + 1) * BLK]
                    pieces.append(jnp.where(mask, piece, NEG))
            live = [piece for piece in pieces if piece is not None]
            top = jnp.max(functools.reduce(jnp.maximum, live), axis=1, keepdims=True)
            top = jnp.maximum(top, merge.top(h, t))
            expos = [None if piece is None else jnp.exp((piece - top) * scale) for piece in pieces]
            total = jnp.sum(sum(e for e in expos if e is not None), axis=1, keepdims=True)
            zero = jnp.zeros((BLK, BLK), BF16)
            parts.append([zero if e is None else e.astype(BF16) for e in expos])
            tops.append(top)
            sums.append(total)
        out = jnp.zeros((2 * BLK, HD), F32)
        for d, (_, v_ref) in enumerate(kvs):
            both = jnp.concatenate(
                [jnp.concatenate(parts[t][2 * d : 2 * d + 2], axis=1) for t in range(2)], axis=0
            )
            out += dot_nn(both, v_ref[:, head(h)])
        for t in range(2):
            merge.store(h, t, tops[t], sums[t], out[t * BLK : (t + 1) * BLK], scale)


class Merge:
    def __init__(self, acc_in, stat_in, acc_out, stat_out):
        self.acc_in, self.stat_in, self.acc_out, self.stat_out = acc_in, stat_in, acc_out, stat_out

    def top(self, h, t):
        return NEG if self.stat_in is None else self.stat_in[t * BLK : (t + 1) * BLK, h : h + 1]

    def store(self, h, t, top, total, out, scale):
        rows = slice(t * BLK, (t + 1) * BLK)
        if self.stat_in is not None:
            fade = jnp.exp((self.top(h, t) - top) * scale)
            total = self.stat_in[rows, 4 + h : 5 + h] * fade + total
            out = self.acc_in[rows, head(h)] * fade + out
        if self.stat_out is None:
            out = out * (1.0 / total)
        else:
            self.stat_out[rows, h : h + 1] = top
            self.stat_out[rows, 4 + h : 5 + h] = total
        self.acc_out[rows, head(h)] = out


def halves(kv_ref):
    return kv_ref.at[: 2 * BLK], kv_ref.at[2 * BLK :]


def inside_kernel(
    list_ref, doc_ref, q_ref, k_ref, v_ref, intra_ref, update_ref, acc_ref, stat_ref
):
    me = lax.axis_index("ctx")
    lane = lax.broadcasted_iota(jnp.int32, (BLK, BLK), 1)
    line = lax.broadcasted_iota(jnp.int32, (BLK, BLK), 0)
    causal = lane <= line
    docs = [doc_row(doc_ref, 2 * me), doc_row(doc_ref, 2 * me + 1)]
    cols = [down(docs[0]), down(docs[1])]
    same = [causal & (cols[t] == docs[t]) for t in range(2)]
    keep = cols[0] == docs[0][:, BLK - 1 :]

    def linear(h, raw):
        for t in range(2):
            rows = slice(t * BLK, (t + 1) * BLK)
            v = v_ref[rows, head(h)]
            scores = jnp.where(same[t], raw[rows, rows], 0.0).astype(BF16)
            intra_ref[rows, head(h)] = dot_nn(scores, v)
            if t == 0:
                kept = jnp.where(keep, v.astype(F32), 0.0).astype(BF16)
                update_ref[head(h), :] = dot_tn(k_ref[rows, head(h)], kept)

    first = Merge(None, None, acc_ref, stat_ref)
    soft_parts(list_ref, doc_ref, q_ref, [(k_ref, v_ref)], (6, 7), first, linear)


def near_kernel(
    list_ref, doc_ref, q_ref, kv1_ref, kv2_ref, acc_in, stat_in, acc_ref, stat_ref
):
    kvs = [halves(kv2_ref), halves(kv1_ref)]
    merge = Merge(acc_in, stat_in, acc_ref, stat_ref)
    soft_parts(list_ref, doc_ref, q_ref, kvs, (2, 3, 4, 5), merge)


def far_kernel(list_ref, doc_ref, q_ref, kv3_ref, acc_in, stat_in, soft_ref):
    merge = Merge(acc_in, stat_in, soft_ref, None)
    soft_parts(list_ref, doc_ref, q_ref, [halves(kv3_ref)], (0, 1), merge)


def mix_kernel(lin_ref, soft_ref, sq_ref, gain_ref, out_ref):
    total = jnp.sum(sq_ref[...], axis=0)
    inverse = lax.rsqrt(total / (HEADS * HD) + 1e-06)
    for t in range(2):
        rows = slice(t * BLK, (t + 1) * BLK)
        col = down(inverse[t : t + 1, :])
        for h in range(4):
            normed = lin_ref[rows, head(h)] * col * gain_ref[:, head(h)]
            out_ref[rows, head(h)] = (normed + soft_ref[rows, head(h)]).astype(BF16)


def local(queries, keys, values, doc_ids, key_blocks, norm_gain):
    tok_rows, feat_width = queries.shape
    devices = lax.axis_size("ctx")
    parts = lax.axis_size("dp")
    docs = doc_ids.reshape(-1, BLK)
    gain = norm_gain.reshape(1, feat_width)
    groups = [list(range(first, first + ROW)) for first in range(0, devices, ROW)]
    wide = pltpu.VMEM((tok_rows, feat_width), F32)

    def shifted(x, by):
        return lax.ppermute(x, "ctx", [(i, i + by) for i in range(devices - by)])

    def exchange(x):
        return lax.all_to_all(x, "ctx", 0, 0, axis_index_groups=groups)

    pieces_shape = pltpu.VMEM((ROW, PIECE, HD), BF16)
    soft_shape = (wide, pltpu.VMEM((tok_rows, HD), F32))
    summary, kv = call(
        summary_kernel,
        (pltpu.VMEM((ROW * PIECE, HD), BF16), pltpu.VMEM((2 * tok_rows, feat_width), BF16)),
        docs,
        keys,
        values,
        scratch=[pltpu.VMEM((8, BLK), jnp.int32), pltpu.SemaphoreType.DMA((3,))],
    )
    kv1 = shifted(kv, 1)
    pieces = exchange(summary.reshape(ROW, PIECE, HD))
    kv2 = shifted(kv1, 1)
    intra, update, *soft = call(
        inside_kernel,
        (wide, pltpu.VMEM((feat_width, HD), F32), *soft_shape),
        key_blocks,
        docs,
        queries,
        keys,
        values,
    )
    total = call(total_kernel, pltpu.VMEM((PIECE, HD), F32), docs, pieces)
    carry = shifted(total, ROW)
    before = call(prefix_kernel, pieces_shape, docs, pieces, carry)
    state = exchange(before).reshape(ROW * PIECE, HD)
    kv3 = shifted(kv2, 1)
    soft = call(
        near_kernel, soft_shape, key_blocks, docs, queries, kv1, kv2, *soft, aliases={5: 0, 6: 1}
    )
    lin, squares = call(
        linear_kernel,
        (wide, pltpu.VMEM((parts, 8, BLK), F32)),
        docs,
        queries,
        intra,
        update,
        state,
        aliases={2: 0},
    )
    squares = lax.all_to_all(squares, "dp", 0, 0)
    soft = call(far_kernel, wide, key_blocks, docs, queries, kv3, *soft, aliases={4: 0})
    return call(
        mix_kernel, jax.ShapeDtypeStruct((tok_rows, feat_width), BF16), lin, soft, squares, gain
    )


def solution(mesh):
    return jax.shard_map(
        local,
        mesh=mesh,
        in_specs=(P("ctx", "dp"), P("ctx", "dp"), P("ctx", "dp"), P(), P("ctx", None), P("dp")),
        out_specs=P("ctx", "dp"),
        check_vma=False,
    )
```

```python
import functools
import math

import jax
import jax.numpy as jnp
from jax import lax
from jax.experimental import pallas as pl
from jax.experimental.pallas import tpu as pltpu
from jax.sharding import PartitionSpec as P


HEADS = 32
HD = 128
BLK = 128
NB = 6
ROW = 24
PIECE = 24
FIRST = 12
NEG = -1e30
F32 = jnp.float32
BF16 = jnp.bfloat16
VM = pl.BlockSpec(memory_space=pltpu.VMEM)
SM = pl.BlockSpec(memory_space=pltpu.SMEM)


def call(body, outs, *operands, scratch=None, aliases=None):
    small = [x.shape == (2, NB) for x in operands]
    if scratch is not None:
        specs = [pl.BlockSpec(memory_space=pltpu.HBM)] * len(operands)
        operands = [pltpu.with_memory_space_constraint(x, pltpu.HBM) for x in operands]
    else:
        specs = [SM if flag else VM for flag in small]
        operands = [
            x if flag else pltpu.with_memory_space_constraint(x, pltpu.VMEM)
            for x, flag in zip(operands, small)
        ]
    return pl.pallas_call(
        body,
        out_shape=outs,
        in_specs=specs,
        out_specs=jax.tree.map(lambda _: VM, outs),
        scratch_shapes=scratch or (),
        input_output_aliases=aliases or {},
        compiler_params=pltpu.CompilerParams(vmem_limit_bytes=12 << 20),
    )(*operands)


def dot_nn(a, b):
    return lax.dot_general(a, b, (((1,), (0,)), ((), ())), preferred_element_type=F32)


def dot_nt(a, b):
    return lax.dot_general(a, b, (((1,), (1,)), ((), ())), preferred_element_type=F32)


def dot_tn(a, b):
    return lax.dot_general(a, b, (((0,), (0,)), ((), ())), preferred_element_type=F32)


def doc_row(doc_ref, row):
    return doc_ref[pl.ds(row, 1), :].astype(F32)


def down(row):
    return jnp.broadcast_to(row, (BLK, BLK)).T


def count_below(row, value):
    return jnp.sum(jnp.where(row < value, 1.0, 0.0), axis=1, keepdims=True)


def head(h):
    return slice(h * HD, (h + 1) * HD)


def summary_kernel(doc_hbm, k_hbm, v_hbm, state_ref, kv_ref, doc_ref, sems):
    me = lax.axis_index("ctx")
    tok = k_hbm.shape[0]
    group = pl.multiple_of((2 * me // 8) * 8, 8)
    copies = [
        pltpu.make_async_copy(doc_hbm.at[pl.ds(group, 8), :], doc_ref, sems.at[0]),
        pltpu.make_async_copy(k_hbm, kv_ref.at[:tok], sems.at[1]),
        pltpu.make_async_copy(v_hbm, kv_ref.at[tok:], sems.at[2]),
    ]
    for copy in copies:
        copy.start()
    state_ref[4 * HD :, :] = jnp.zeros((ROW * PIECE - 4 * HD, HD), BF16)
    copies[0].wait()
    d0, d1 = doc_row(doc_ref, 2 * me - group), doc_row(doc_ref, 2 * me - group + 1)
    last = d1[:, BLK - 1 :]
    first = count_below(d0, last) + count_below(d1, last)
    rows = lax.broadcasted_iota(jnp.int32, (tok, HD), 0).astype(F32)
    keep = rows >= first
    copies[1].wait()
    copies[2].wait()
    for h in range(4):
        vm = jnp.where(keep, kv_ref[tok:, head(h)].astype(F32), 0.0).astype(BF16)
        state_ref[head(h), :] = dot_tn(kv_ref[:tok, head(h)], vm).astype(BF16)


def row_docs(doc_ref):
    row = lax.axis_index("ctx") // ROW
    docs = doc_ref[pl.ds(pl.multiple_of(row * 2 * ROW, 8), 2 * ROW), :].astype(F32)
    return row, jnp.broadcast_to(docs[:, BLK - 1 :], (2 * ROW, HD))


def place(j):
    return (j - FIRST) % ROW


def total_kernel(doc_ref, piece_ref, total_ref):
    _, docs = row_docs(doc_ref)
    last = docs[2 * ROW - 1 :, :]
    total = jnp.zeros((PIECE, HD), F32)
    for j in range(ROW):
        same = docs[2 * j + 1 : 2 * j + 2, :] == last
        total += jnp.where(same, piece_ref[place(j)].astype(F32), 0.0)
    total_ref[...] = total


def prefix_kernel(doc_ref, piece_ref, carry_ref, before_ref):
    row, docs = row_docs(doc_ref)
    past = doc_row(doc_ref, jnp.maximum(2 * ROW * row - 1, 0))
    before = jnp.broadcast_to(past[:, BLK - 1 :], (1, HD))
    running = carry_ref[...]
    for j in range(ROW):
        before_ref[place(j)] = running.astype(BF16)
        now = docs[2 * j + 1 : 2 * j + 2, :]
        running = jnp.where(now == before, running, 0.0) + piece_ref[place(j)].astype(F32)
        before = now


def linear_kernel(doc_ref, q_ref, intra_ref, update_ref, state_ref, lin_ref, sq_ref):
    me = lax.axis_index("ctx")
    past = doc_row(doc_ref, jnp.maximum(2 * me - 1, 0))[:, BLK - 1 :]
    docs = [doc_row(doc_ref, 2 * me), doc_row(doc_ref, 2 * me + 1)]
    mid = docs[0][:, BLK - 1 :]
    live = [down(docs[0]) == past, down(docs[1]) == mid]
    squares = [jnp.zeros((BLK, HD), F32), jnp.zeros((BLK, HD), F32)]
    for h in range(4):
        first = state_ref[head(h), :]
        second = (jnp.where(past == mid, first.astype(F32), 0.0) + update_ref[head(h), :]).astype(BF16)
        for t, state in enumerate((first, second)):
            rows = slice(t * BLK, (t + 1) * BLK)
            inner = jnp.where(live[t], dot_nn(q_ref[rows, head(h)], state), 0.0)
            lin = inner + intra_ref[rows, head(h)]
            lin_ref[rows, head(h)] = lin
            squares[t] += lin * lin
    sums = [jnp.sum(square.T, axis=0, keepdims=True) for square in squares]
    row = lax.broadcasted_iota(jnp.int32, (8, BLK), 0)
    tile = jnp.where(row == 0, sums[0], jnp.where(row == 1, sums[1], 0.0))
    for part in range(sq_ref.shape[0]):
        sq_ref[part] = tile


def soft_parts(list_ref, doc_ref, q_ref, kvs, windows, merge, own=None):
    me = lax.axis_index("ctx")
    base = 2 * me - NB
    lane = lax.broadcasted_iota(jnp.int32, (BLK, BLK), 1)
    line = lax.broadcasted_iota(jnp.int32, (BLK, BLK), 0)
    causal = lane <= line
    scale = 1.0 / math.sqrt(HD)
    masks = []
    for t in range(2):
        col = down(doc_row(doc_ref, base + NB + t))
        mine = []
        for w in windows:
            if w < t or w > NB + t:
                mine.append(None)
                continue
            block = base + w
            listed = list_ref[t, 0] == block
            for n in range(1, NB):
                listed = listed | (list_ref[t, n] == block)
            listed = listed & (block >= 0)
            row = doc_row(doc_ref, jnp.maximum(block, 0))
            match = col == jnp.where(listed, row, -1.0)
            mine.append(match & causal if w == NB + t else match)
        masks.append(mine)
    for h in range(4):
        q = q_ref[:, head(h)]
        raw = [dot_nt(q, k_ref[:, head(h)]) for k_ref, _ in kvs]
        if own is not None:
            own(h, raw[0])
        tops, sums, parts = [], [], []
        for t in range(2):
            rows = slice(t * BLK, (t + 1) * BLK)
            pieces = []
            for n, mask in enumerate(masks[t]):
                if mask is None:
                    pieces.append(None)
                else:
                    piece = raw[n // 2][rows, (n % 2) * BLK : (n % 2 + 1) * BLK]
                    pieces.append(jnp.where(mask, piece, NEG))
            live = [piece for piece in pieces if piece is not None]
            top = jnp.max(functools.reduce(jnp.maximum, live), axis=1, keepdims=True)
            top = jnp.maximum(top, merge.top(h, t))
            expos = [None if piece is None else jnp.exp((piece - top) * scale) for piece in pieces]
            total = jnp.sum(sum(e for e in expos if e is not None), axis=1, keepdims=True)
            zero = jnp.zeros((BLK, BLK), BF16)
            parts.append([zero if e is None else e.astype(BF16) for e in expos])
            tops.append(top)
            sums.append(total)
        out = jnp.zeros((2 * BLK, HD), F32)
        for d, (_, v_ref) in enumerate(kvs):
            both = jnp.concatenate(
                [jnp.concatenate(parts[t][2 * d : 2 * d + 2], axis=1) for t in range(2)], axis=0
            )
            out += dot_nn(both, v_ref[:, head(h)])
        for t in range(2):
            merge.store(h, t, tops[t], sums[t], out[t * BLK : (t + 1) * BLK], scale)


class Merge:
    def __init__(self, acc_in, stat_in, acc_out, stat_out):
        self.acc_in, self.stat_in, self.acc_out, self.stat_out = acc_in, stat_in, acc_out, stat_out

    def top(self, h, t):
        return NEG if self.stat_in is None else self.stat_in[t * BLK : (t + 1) * BLK, h : h + 1]

    def store(self, h, t, top, total, out, scale):
        rows = slice(t * BLK, (t + 1) * BLK)
        if self.stat_in is not None:
            fade = jnp.exp((self.top(h, t) - top) * scale)
            total = self.stat_in[rows, 4 + h : 5 + h] * fade + total
            out = self.acc_in[rows, head(h)] * fade + out
        if self.stat_out is None:
            out = out * (1.0 / total)
        else:
            self.stat_out[rows, h : h + 1] = top
            self.stat_out[rows, 4 + h : 5 + h] = total
        self.acc_out[rows, head(h)] = out


def halves(kv_ref):
    return kv_ref.at[: 2 * BLK], kv_ref.at[2 * BLK :]


def inside_kernel(
    list_ref, doc_ref, q_ref, k_ref, v_ref, intra_ref, update_ref, acc_ref, stat_ref
):
    me = lax.axis_index("ctx")
    lane = lax.broadcasted_iota(jnp.int32, (BLK, BLK), 1)
    line = lax.broadcasted_iota(jnp.int32, (BLK, BLK), 0)
    causal = lane <= line
    docs = [doc_row(doc_ref, 2 * me), doc_row(doc_ref, 2 * me + 1)]
    cols = [down(docs[0]), down(docs[1])]
    same = [causal & (cols[t] == docs[t]) for t in range(2)]
    keep = cols[0] == docs[0][:, BLK - 1 :]

    def linear(h, raw):
        for t in range(2):
            rows = slice(t * BLK, (t + 1) * BLK)
            v = v_ref[rows, head(h)]
            scores = jnp.where(same[t], raw[rows, rows], 0.0).astype(BF16)
            intra_ref[rows, head(h)] = dot_nn(scores, v)
            if t == 0:
                kept = jnp.where(keep, v.astype(F32), 0.0).astype(BF16)
                update_ref[head(h), :] = dot_tn(k_ref[rows, head(h)], kept)

    first = Merge(None, None, acc_ref, stat_ref)
    soft_parts(list_ref, doc_ref, q_ref, [(k_ref, v_ref)], (6, 7), first, linear)


def near_kernel(
    list_ref, doc_ref, q_ref, kv1_ref, kv2_ref, acc_in, stat_in, acc_ref, stat_ref
):
    kvs = [halves(kv2_ref), halves(kv1_ref)]
    merge = Merge(acc_in, stat_in, acc_ref, stat_ref)
    soft_parts(list_ref, doc_ref, q_ref, kvs, (2, 3, 4, 5), merge)


def far_kernel(list_ref, doc_ref, q_ref, kv3_ref, acc_in, stat_in, soft_ref):
    merge = Merge(acc_in, stat_in, soft_ref, None)
    soft_parts(list_ref, doc_ref, q_ref, [halves(kv3_ref)], (0, 1), merge)


def mix_kernel(lin_ref, soft_ref, sq_ref, gain_ref, out_ref):
    total = jnp.sum(sq_ref[...], axis=0)
    inverse = lax.rsqrt(total / (HEADS * HD) + 1e-06)
    for t in range(2):
        rows = slice(t * BLK, (t + 1) * BLK)
        col = down(inverse[t : t + 1, :])
        for h in range(4):
            normed = lin_ref[rows, head(h)] * col * gain_ref[:, head(h)]
            out_ref[rows, head(h)] = (normed + soft_ref[rows, head(h)]).astype(BF16)


def local(queries, keys, values, doc_ids, key_blocks, norm_gain):
    tok_rows, feat_width = queries.shape
    devices = lax.axis_size("ctx")
    parts = lax.axis_size("dp")
    docs = doc_ids.reshape(-1, BLK)
    gain = norm_gain.reshape(1, feat_width)
    groups = [
        [first + (n + FIRST) % ROW for n in range(ROW)] for first in range(0, devices, ROW)
    ]
    wide = pltpu.VMEM((tok_rows, feat_width), F32)

    def shifted(x, by):
        return lax.ppermute(x, "ctx", [(i, i + by) for i in range(devices - by)])

    def exchange(x):
        return lax.all_to_all(x, "ctx", 0, 0, axis_index_groups=groups)

    pieces_shape = pltpu.VMEM((ROW, PIECE, HD), BF16)
    soft_shape = (wide, pltpu.VMEM((tok_rows, HD), F32))
    summary, kv = call(
        summary_kernel,
        (pltpu.VMEM((ROW * PIECE, HD), BF16), pltpu.VMEM((2 * tok_rows, feat_width), BF16)),
        docs,
        keys,
        values,
        scratch=[pltpu.VMEM((8, BLK), jnp.int32), pltpu.SemaphoreType.DMA((3,))],
    )
    kv1 = shifted(kv, 1)
    pieces = exchange(summary.reshape(ROW, PIECE, HD))
    kv2 = shifted(kv1, 1)
    intra, update, *soft = call(
        inside_kernel,
        (wide, pltpu.VMEM((feat_width, HD), F32), *soft_shape),
        key_blocks,
        docs,
        queries,
        keys,
        values,
    )
    total = call(total_kernel, pltpu.VMEM((PIECE, HD), F32), docs, pieces)
    carry = shifted(total, ROW)
    before = call(prefix_kernel, pieces_shape, docs, pieces, carry)
    state = exchange(before).reshape(ROW * PIECE, HD)
    kv3 = shifted(kv2, 1)
    soft = call(
        near_kernel, soft_shape, key_blocks, docs, queries, kv1, kv2, *soft, aliases={5: 0, 6: 1}
    )
    lin, squares = call(
        linear_kernel,
        (wide, pltpu.VMEM((parts, 8, BLK), F32)),
        docs,
        queries,
        intra,
        update,
        state,
        aliases={2: 0},
    )
    squares = lax.all_to_all(squares, "dp", 0, 0)
    soft = call(far_kernel, wide, key_blocks, docs, queries, kv3, *soft, aliases={4: 0})
    return call(
        mix_kernel, jax.ShapeDtypeStruct((tok_rows, feat_width), BF16), lin, soft, squares, gain
    )


def solution(mesh):
    return jax.shard_map(
        local,
        mesh=mesh,
        in_specs=(P("ctx", "dp"), P("ctx", "dp"), P("ctx", "dp"), P(), P("ctx", None), P("dp")),
        out_specs=P("ctx", "dp"),
        check_vma=False,
    )
```

```python
import functools
import math

import jax
import jax.numpy as jnp
from jax import lax
from jax.experimental import pallas as pl
from jax.experimental.pallas import tpu as pltpu
from jax.sharding import PartitionSpec as P


HEADS = 32
HD = 128
BLK = 128
NB = 6
ROW = 24
PIECE = 24
FIRST = 15
LEAD = 6
NEG = -1e30
F32 = jnp.float32
BF16 = jnp.bfloat16
VM = pl.BlockSpec(memory_space=pltpu.VMEM)
SM = pl.BlockSpec(memory_space=pltpu.SMEM)


def call(body, outs, *operands, scratch=None, aliases=None):
    small = [x.shape == (2, NB) for x in operands]
    if scratch is not None:
        specs = [pl.BlockSpec(memory_space=pltpu.HBM)] * len(operands)
        operands = [pltpu.with_memory_space_constraint(x, pltpu.HBM) for x in operands]
    else:
        specs = [SM if flag else VM for flag in small]
        operands = [
            x if flag else pltpu.with_memory_space_constraint(x, pltpu.VMEM)
            for x, flag in zip(operands, small)
        ]
    return pl.pallas_call(
        body,
        out_shape=outs,
        in_specs=specs,
        out_specs=jax.tree.map(lambda _: VM, outs),
        scratch_shapes=scratch or (),
        input_output_aliases=aliases or {},
        compiler_params=pltpu.CompilerParams(vmem_limit_bytes=12 << 20),
    )(*operands)


def dot_nn(a, b):
    return lax.dot_general(a, b, (((1,), (0,)), ((), ())), preferred_element_type=F32)


def dot_nt(a, b):
    return lax.dot_general(a, b, (((1,), (1,)), ((), ())), preferred_element_type=F32)


def dot_tn(a, b):
    return lax.dot_general(a, b, (((0,), (0,)), ((), ())), preferred_element_type=F32)


def doc_row(doc_ref, row):
    return doc_ref[pl.ds(row, 1), :].astype(F32)


def down(row):
    return jnp.broadcast_to(row, (BLK, BLK)).T


def count_below(row, value):
    return jnp.sum(jnp.where(row < value, 1.0, 0.0), axis=1, keepdims=True)


def head(h):
    return slice(h * HD, (h + 1) * HD)


def summary_kernel(doc_hbm, k_hbm, v_hbm, state_ref, kv_ref, doc_ref, sems):
    me = lax.axis_index("ctx")
    tok = k_hbm.shape[0]
    group = pl.multiple_of((2 * me // 8) * 8, 8)
    copies = [
        pltpu.make_async_copy(doc_hbm.at[pl.ds(group, 8), :], doc_ref, sems.at[0]),
        pltpu.make_async_copy(k_hbm, kv_ref.at[:tok], sems.at[1]),
        pltpu.make_async_copy(v_hbm, kv_ref.at[tok:], sems.at[2]),
    ]
    for copy in copies:
        copy.start()
    state_ref[4 * HD :, :] = jnp.zeros((ROW * PIECE - 4 * HD, HD), BF16)
    copies[0].wait()
    d0, d1 = doc_row(doc_ref, 2 * me - group), doc_row(doc_ref, 2 * me - group + 1)
    last = d1[:, BLK - 1 :]
    first = count_below(d0, last) + count_below(d1, last)
    rows = lax.broadcasted_iota(jnp.int32, (tok, HD), 0).astype(F32)
    keep = rows >= first
    copies[1].wait()
    copies[2].wait()
    for h in range(4):
        vm = jnp.where(keep, kv_ref[tok:, head(h)].astype(F32), 0.0).astype(BF16)
        state_ref[head(h), :] = dot_tn(kv_ref[:tok, head(h)], vm).astype(BF16)


def row_docs(doc_ref):
    row = lax.axis_index("ctx") // ROW
    docs = doc_ref[pl.ds(pl.multiple_of(row * 2 * ROW, 8), 2 * ROW), :].astype(F32)
    return row, jnp.broadcast_to(docs[:, BLK - 1 :], (2 * ROW, HD))


def place(j):
    return (j - FIRST) % ROW


def total_kernel(doc_ref, piece_ref, total_ref):
    _, docs = row_docs(doc_ref)
    last = docs[2 * ROW - 1 :, :]
    total = jnp.zeros((PIECE, HD), F32)
    for j in range(ROW):
        same = docs[2 * j + 1 : 2 * j + 2, :] == last
        total += jnp.where(same, piece_ref[place(j)].astype(F32), 0.0)
    total_ref[...] = total


def prefix_kernel(doc_ref, piece_ref, carry_ref, before_ref):
    row, docs = row_docs(doc_ref)
    past = doc_row(doc_ref, jnp.maximum(2 * ROW * row - 1, 0))
    before = jnp.broadcast_to(past[:, BLK - 1 :], (1, HD))
    running = carry_ref[...]
    for j in range(ROW):
        before_ref[place(j)] = running.astype(BF16)
        now = docs[2 * j + 1 : 2 * j + 2, :]
        running = jnp.where(now == before, running, 0.0) + piece_ref[place(j)].astype(F32)
        before = now


def linear_kernel(doc_ref, q_ref, intra_ref, update_ref, state_ref, lin_ref, sq_ref):
    me = lax.axis_index("ctx")
    past = doc_row(doc_ref, jnp.maximum(2 * me - 1, 0))[:, BLK - 1 :]
    docs = [doc_row(doc_ref, 2 * me), doc_row(doc_ref, 2 * me + 1)]
    mid = docs[0][:, BLK - 1 :]
    live = [down(docs[0]) == past, down(docs[1]) == mid]
    squares = [jnp.zeros((BLK, HD), F32), jnp.zeros((BLK, HD), F32)]
    for h in range(4):
        first = state_ref[head(h), :]
        second = (jnp.where(past == mid, first.astype(F32), 0.0) + update_ref[head(h), :]).astype(BF16)
        for t, state in enumerate((first, second)):
            rows = slice(t * BLK, (t + 1) * BLK)
            inner = jnp.where(live[t], dot_nn(q_ref[rows, head(h)], state), 0.0)
            lin = inner + intra_ref[rows, head(h)]
            lin_ref[rows, head(h)] = lin
            squares[t] += lin * lin
    sums = [jnp.sum(square.T, axis=0, keepdims=True) for square in squares]
    row = lax.broadcasted_iota(jnp.int32, (8, BLK), 0)
    tile = jnp.where(row == 0, sums[0], jnp.where(row == 1, sums[1], 0.0))
    for part in range(sq_ref.shape[0]):
        sq_ref[part] = tile


def soft_parts(list_ref, doc_ref, q_ref, kvs, windows, merge, own=None):
    me = lax.axis_index("ctx")
    base = 2 * me - NB
    lane = lax.broadcasted_iota(jnp.int32, (BLK, BLK), 1)
    line = lax.broadcasted_iota(jnp.int32, (BLK, BLK), 0)
    causal = lane <= line
    scale = 1.0 / math.sqrt(HD)
    masks = []
    for t in range(2):
        col = down(doc_row(doc_ref, base + NB + t))
        mine = []
        for w in windows:
            if w < t or w > NB + t:
                mine.append(None)
                continue
            block = base + w
            listed = list_ref[t, 0] == block
            for n in range(1, NB):
                listed = listed | (list_ref[t, n] == block)
            listed = listed & (block >= 0)
            row = doc_row(doc_ref, jnp.maximum(block, 0))
            match = col == jnp.where(listed, row, -1.0)
            mine.append(match & causal if w == NB + t else match)
        masks.append(mine)
    for h in range(4):
        q = q_ref[:, head(h)]
        raw = [dot_nt(q, k_ref[:, head(h)]) for k_ref, _ in kvs]
        if own is not None:
            own(h, raw[0])
        tops, sums, parts = [], [], []
        for t in range(2):
            rows = slice(t * BLK, (t + 1) * BLK)
            pieces = []
            for n, mask in enumerate(masks[t]):
                if mask is None:
                    pieces.append(None)
                else:
                    piece = raw[n // 2][rows, (n % 2) * BLK : (n % 2 + 1) * BLK]
                    pieces.append(jnp.where(mask, piece, NEG))
            live = [piece for piece in pieces if piece is not None]
            top = jnp.max(functools.reduce(jnp.maximum, live), axis=1, keepdims=True)
            top = jnp.maximum(top, merge.top(h, t))
            expos = [None if piece is None else jnp.exp((piece - top) * scale) for piece in pieces]
            total = jnp.sum(sum(e for e in expos if e is not None), axis=1, keepdims=True)
            zero = jnp.zeros((BLK, BLK), BF16)
            parts.append([zero if e is None else e.astype(BF16) for e in expos])
            tops.append(top)
            sums.append(total)
        out = jnp.zeros((2 * BLK, HD), F32)
        for d, (_, v_ref) in enumerate(kvs):
            both = jnp.concatenate(
                [jnp.concatenate(parts[t][2 * d : 2 * d + 2], axis=1) for t in range(2)], axis=0
            )
            out += dot_nn(both, v_ref[:, head(h)])
        for t in range(2):
            merge.store(h, t, tops[t], sums[t], out[t * BLK : (t + 1) * BLK], scale)


class Merge:
    def __init__(self, acc_in, stat_in, acc_out, stat_out):
        self.acc_in, self.stat_in, self.acc_out, self.stat_out = acc_in, stat_in, acc_out, stat_out

    def top(self, h, t):
        return NEG if self.stat_in is None else self.stat_in[t * BLK : (t + 1) * BLK, h : h + 1]

    def store(self, h, t, top, total, out, scale):
        rows = slice(t * BLK, (t + 1) * BLK)
        if self.stat_in is not None:
            fade = jnp.exp((self.top(h, t) - top) * scale)
            total = self.stat_in[rows, 4 + h : 5 + h] * fade + total
            out = self.acc_in[rows, head(h)] * fade + out
        if self.stat_out is None:
            out = out * (1.0 / total)
        else:
            self.stat_out[rows, h : h + 1] = top
            self.stat_out[rows, 4 + h : 5 + h] = total
        self.acc_out[rows, head(h)] = out


def halves(kv_ref):
    return kv_ref.at[: 2 * BLK], kv_ref.at[2 * BLK :]


def inside_kernel(
    list_ref, doc_ref, q_ref, k_ref, v_ref, intra_ref, update_ref, acc_ref, stat_ref
):
    me = lax.axis_index("ctx")
    lane = lax.broadcasted_iota(jnp.int32, (BLK, BLK), 1)
    line = lax.broadcasted_iota(jnp.int32, (BLK, BLK), 0)
    causal = lane <= line
    docs = [doc_row(doc_ref, 2 * me), doc_row(doc_ref, 2 * me + 1)]
    cols = [down(docs[0]), down(docs[1])]
    same = [causal & (cols[t] == docs[t]) for t in range(2)]
    keep = cols[0] == docs[0][:, BLK - 1 :]

    def linear(h, raw):
        for t in range(2):
            rows = slice(t * BLK, (t + 1) * BLK)
            v = v_ref[rows, head(h)]
            scores = jnp.where(same[t], raw[rows, rows], 0.0).astype(BF16)
            intra_ref[rows, head(h)] = dot_nn(scores, v)
            if t == 0:
                kept = jnp.where(keep, v.astype(F32), 0.0).astype(BF16)
                update_ref[head(h), :] = dot_tn(k_ref[rows, head(h)], kept)

    first = Merge(None, None, acc_ref, stat_ref)
    soft_parts(list_ref, doc_ref, q_ref, [(k_ref, v_ref)], (6, 7), first, linear)


def near_kernel(
    list_ref, doc_ref, q_ref, kv1_ref, kv2_ref, acc_in, stat_in, acc_ref, stat_ref
):
    kvs = [halves(kv2_ref), halves(kv1_ref)]
    merge = Merge(acc_in, stat_in, acc_ref, stat_ref)
    soft_parts(list_ref, doc_ref, q_ref, kvs, (2, 3, 4, 5), merge)


def far_kernel(list_ref, doc_ref, q_ref, kv3_ref, acc_in, stat_in, soft_ref):
    merge = Merge(acc_in, stat_in, soft_ref, None)
    soft_parts(list_ref, doc_ref, q_ref, [halves(kv3_ref)], (0, 1), merge)


def mix_kernel(lin_ref, soft_ref, sq_ref, gain_ref, out_ref):
    total = jnp.sum(sq_ref[...], axis=0)
    inverse = lax.rsqrt(total / (HEADS * HD) + 1e-06)
    for t in range(2):
        rows = slice(t * BLK, (t + 1) * BLK)
        col = down(inverse[t : t + 1, :])
        for h in range(4):
            normed = lin_ref[rows, head(h)] * col * gain_ref[:, head(h)]
            out_ref[rows, head(h)] = (normed + soft_ref[rows, head(h)]).astype(BF16)


def local(queries, keys, values, doc_ids, key_blocks, norm_gain):
    tok_rows, feat_width = queries.shape
    devices = lax.axis_size("ctx")
    parts = lax.axis_size("dp")
    docs = doc_ids.reshape(-1, BLK)
    gain = norm_gain.reshape(1, feat_width)
    groups = [
        [first + (n + FIRST) % ROW for n in range(ROW)] for first in range(0, devices, ROW)
    ]
    wide = pltpu.VMEM((tok_rows, feat_width), F32)

    def shifted(x, by):
        return lax.ppermute(x, "ctx", [(i, i + by) for i in range(devices - by)])

    def exchange(x):
        return lax.all_to_all(x, "ctx", 0, 0, axis_index_groups=groups)

    pieces_shape = pltpu.VMEM((ROW, PIECE, HD), BF16)
    soft_shape = (wide, pltpu.VMEM((tok_rows, HD), F32))
    summary, kv = call(
        summary_kernel,
        (pltpu.VMEM((ROW * PIECE, HD), BF16), pltpu.VMEM((2 * tok_rows, feat_width), BF16)),
        docs,
        keys,
        values,
        scratch=[pltpu.VMEM((8, BLK), jnp.int32), pltpu.SemaphoreType.DMA((3,))],
    )
    kv1 = shifted(kv, 1)
    pieces = exchange(summary.reshape(ROW, PIECE, HD))
    kv2 = shifted(kv1, 1)
    intra, update, *soft = call(
        inside_kernel,
        (wide, pltpu.VMEM((feat_width, HD), F32), *soft_shape),
        key_blocks,
        docs,
        queries,
        keys,
        values,
    )
    total = call(total_kernel, pltpu.VMEM((PIECE, HD), F32), docs, pieces)
    carry = shifted(total, ROW)
    before = call(prefix_kernel, pieces_shape, docs, pieces, carry)
    state = exchange(before).reshape(ROW * PIECE, HD)
    kv3 = shifted(kv2, 1)
    soft = call(
        near_kernel, soft_shape, key_blocks, docs, queries, kv1, kv2, *soft, aliases={5: 0, 6: 1}
    )
    lin, squares = call(
        linear_kernel,
        (wide, pltpu.VMEM((parts, 8, BLK), F32)),
        docs,
        queries,
        intra,
        update,
        state,
        aliases={2: 0},
    )
    order = [[(LEAD + n) % parts for n in range(parts)]]
    squares = lax.all_to_all(squares, "dp", 0, 0, axis_index_groups=order)
    soft = call(far_kernel, wide, key_blocks, docs, queries, kv3, *soft, aliases={4: 0})
    return call(
        mix_kernel, jax.ShapeDtypeStruct((tok_rows, feat_width), BF16), lin, soft, squares, gain
    )


def solution(mesh):
    return jax.shard_map(
        local,
        mesh=mesh,
        in_specs=(P("ctx", "dp"), P("ctx", "dp"), P("ctx", "dp"), P(), P("ctx", None), P("dp")),
        out_specs=P("ctx", "dp"),
        check_vma=False,
    )
```
